512 devices in a mesh: space: 128 (over z, y, x_lo), shot: 4 (over x_hi, core).
Axes of the slice: x: 4 (x_hi: 2, x_lo: 2; x = x_hi * 2 + x_lo), y: 4, z: 16, core: 2. Of those that a mesh axis runs over, the one named last changes fastest.
Arguments:
- velocity: float32 [1024, 192, 128], P('space'), may hold values from 1.5 to 4.5
- wave_now: float32 [4, 1024, 192, 128], P('shot', 'space'), may hold values from -6 to 6
- wave_prev: float32 [4, 1024, 192, 128], P('shot', 'space'), may hold values from -6 to 6
- adjoint_now: float32 [4, 1024, 192, 128], P('shot', 'space'), may hold values from -6 to 6
- adjoint_prev: float32 [4, 1024, 192, 128], P('shot', 'space'), may hold values from -6 to 6
- source_cells: int32 [4, 128], P('shot'), may hold values from 0 to 25165823, as said below
- wavelet: float32 [4, 10, 128], P('shot'), may hold values from -24 to 24
- receiver_cells: int32 [65536], P('space'), may hold values from 0 to 196607, as said below
- receiver_counts: int32 [128], P('space'), may hold values from 128 to 512, as said below
- observed: float32 [4, 10, 65536], P('shot', None, 'space'), may hold values from -24 to 24
Outputs:
- gradient: float32 [1024, 192, 128], P('space', 'shot')
The draws below stay inside these ranges and needn't reach their ends.
Inputs may be any that keep to these rules, and one draw needn't show every extreme that they name: `source_cells`: flat indices into the whole grid (first dimension slowest); the 128 cells of one shot group are distinct. `receiver_cells`: flat indices within one device's block of 8 x 192 x 128 cells (first dimension slowest); the 512 cells of one block are distinct. `receiver_counts`: the live slots of a block come first.
All inputs are finite; a program needn't handle non-finite values.
Results may differ from the reference program's by a relative error of at most 0.00002.
Values sent between devices are 32-bit elements; how exact they have to be, the bound alone decides.
No kernel may reach another device: no remote copies, remote signals or barrier semaphores. Data moves between devices by JAX's collectives and lax.ppermute only.
A program may use at most 64 MiB of HBM per device.

```python
import jax
import jax.numpy as jnp
from jax import lax

CX = 8
NY = 192
NZ = 128
STEPS = 10
NSRC = 128
RB = 512
SHOTS = 4
SLABS = 128
NX = 1024
RECS = 65536


def draw_source_cells(key, part):
    stride = NX * NY * NZ // NSRC
    baseline = jnp.arange(NSRC, dtype=jnp.int32) * stride
    jitter = jax.random.randint(jax.random.fold_in(key, 11), (SHOTS, NSRC), 0, stride, dtype=jnp.int32)
    return baseline[None, :] + jitter


def draw_receiver_cells(key, part):
    stride = CX * NY * NZ // RB
    slot_ids = jnp.arange(RECS, dtype=jnp.int32) % RB
    jitter = jax.random.randint(jax.random.fold_in(key, 12), (RECS,), 0, stride, dtype=jnp.int32)
    return slot_ids * stride + jitter


def draw_receiver_counts(key, part):
    baseline = jax.random.randint(jax.random.fold_in(key, 13), (SLABS,), RB // 4, RB + 1, dtype=jnp.int32)
    fullest = jax.random.randint(jax.random.fold_in(key, 14), (), 0, SLABS, dtype=jnp.int32)
    lowest = (fullest + 1 + jax.random.randint(jax.random.fold_in(key, 15), (), 0, SLABS - 1, dtype=jnp.int32)) % SLABS
    slab_ids = jnp.arange(SLABS, dtype=jnp.int32)
    return jnp.where(slab_ids == fullest, RB, jnp.where(slab_ids == lowest, RB // 4, baseline)).astype(jnp.int32)


def shard_levels(stream_key, extent, split, smallest, largest):
    def one(axis_at, parts):
        heights = jax.random.uniform(jax.random.fold_in(jax.random.fold_in(stream_key, 6), axis_at), (parts,), jnp.float32, smallest / len(split), largest / len(split))
        return jnp.repeat(jnp.exp(heights), extent[axis_at] // parts).reshape((-1,) + (1,) * (len(extent) - axis_at - 1))

    loudness = one(*split[0])
    for cut in split[1:]:
        loudness = loudness * one(*cut)
    return loudness


def normal_values(own_key, shape, width, bound, shards=(), kind=jnp.bfloat16):
    drawn = width * jax.random.normal(own_key, shape, jnp.float32)
    if shards:
        drawn = drawn * shard_levels(own_key, shape, shards, -0.22, 0.18)
    return jnp.clip(drawn, -bound, bound).astype(kind)


def setup_inputs(seed: int = 0) -> dict:
    seeds = jax.random.split(jax.random.key(seed), 11)
    velocity = jnp.clip(1.5 + 3.0 * jax.random.uniform(seeds[0], (NX, NY, NZ), jnp.float32) ** shard_levels(seeds[0], (NX, NY, NZ), ((0, 128),), -0.2, 0.2), 1.5, 4.5)
    wave_now = normal_values(seeds[1], (SHOTS, NX, NY, NZ), 1.0, 6.0, ((0, 4), (1, 128)), jnp.float32)
    wave_prev = normal_values(seeds[2], (SHOTS, NX, NY, NZ), 1.0, 6.0, ((0, 4), (1, 128)), jnp.float32)
    adjoint_now = normal_values(seeds[3], (SHOTS, NX, NY, NZ), 1.0, 6.0, ((0, 4), (1, 128)), jnp.float32)
    adjoint_prev = normal_values(seeds[4], (SHOTS, NX, NY, NZ), 1.0, 6.0, ((0, 4), (1, 128)), jnp.float32)
    source_cells = draw_source_cells(jax.random.fold_in(seeds[10], 71), 0)
    wavelet = normal_values(seeds[6], (SHOTS, STEPS, NSRC), 4.0, 24.0, ((0, 4),), jnp.float32)
    receiver_cells = draw_receiver_cells(jax.random.fold_in(seeds[10], 71), 0)
    receiver_counts = draw_receiver_counts(jax.random.fold_in(seeds[10], 71), 0)
    observed = normal_values(seeds[9], (SHOTS, STEPS, RECS), 4.0, 24.0, ((0, 4), (2, 128)), jnp.float32)
    return {"velocity": velocity, "wave_now": wave_now, "wave_prev": wave_prev, "adjoint_now": adjoint_now, "adjoint_prev": adjoint_prev, "source_cells": source_cells, "wavelet": wavelet, "receiver_cells": receiver_cells, "receiver_counts": receiver_counts, "observed": observed}


TAPS = (-205.0 / 72.0, 8.0 / 5.0, -1.0 / 5.0, 8.0 / 315.0, -1.0 / 560.0)
COURANT = 0.09


def laplace(widened):
    length_x = widened.shape[0] - 8
    extent_y = widened.shape[1]
    extent_z = widened.shape[2]
    padded = jnp.pad(widened, ((0, 0), (4, 4), (4, 4)))
    centre = widened[4:4 + length_x]
    result = (3.0 * TAPS[0]) * centre
    for distance in range(1, 5):
        beside_all = padded[4 + distance:4 + distance + length_x, 4:4 + extent_y, 4:4 + extent_z] + padded[4 - distance:4 - distance + length_x, 4:4 + extent_y, 4:4 + extent_z]
        beside_all = beside_all + padded[4:4 + length_x, 4 + distance:4 + distance + extent_y, 4:4 + extent_z] + padded[4:4 + length_x, 4 - distance:4 - distance + extent_y, 4:4 + extent_z]
        beside_all = beside_all + padded[4:4 + length_x, 4:4 + extent_y, 4 + distance:4 + distance + extent_z] + padded[4:4 + length_x, 4:4 + extent_y, 4 - distance:4 - distance + extent_z]
        result = result + TAPS[distance] * beside_all
    return result


def one_shot(courant_sq, shot_inputs, receiver_index, live_slots):
    start_now, start_prev, adjoint_start, adjoint_after, source_index, pulses, observed_shot = shot_inputs
    shape_grid = start_now.shape

    def forward(carried, source_pulse):
        current, former = carried
        widened = jnp.pad(current, ((4, 4), (0, 0), (0, 0)))
        latest = 2.0 * current - former + courant_sq * laplace(widened)
        latest = latest.reshape(-1).at[source_index].add(source_pulse).reshape(shape_grid)
        acceleration = latest - 2.0 * current + former
        return (latest, current), (acceleration, latest.reshape(-1)[receiver_index])

    _, (accelerations, traces) = lax.scan(forward, (start_now, start_prev), pulses)
    misfit = (traces - observed_shot) * live_slots

    def backward(carried, inputs):
        following, furthest, imaging = carried
        acceleration, residual = inputs
        widened = jnp.pad(following, ((4, 4), (0, 0), (0, 0)))
        earlier = 2.0 * following - furthest + courant_sq * laplace(widened)
        earlier = earlier.reshape(-1).at[receiver_index].add(residual).reshape(shape_grid)
        return (earlier, following, imaging + earlier * acceleration), None

    empty_field = jnp.zeros(shape_grid, jnp.float32)
    (_, _, imaging), _ = lax.scan(backward, (adjoint_start, adjoint_after, empty_field), (accelerations, misfit), reverse=True)
    return imaging


def reference(velocity, wave_now, wave_prev, adjoint_now, adjoint_prev, source_cells, wavelet, receiver_cells, receiver_counts, observed):
    courant_sq = (COURANT * velocity) ** 2
    slot_ids = jnp.arange(RECS, dtype=jnp.int32)
    owner_slab = slot_ids // RB
    receiver_index = (owner_slab * (CX * NY * NZ) + receiver_cells).astype(jnp.int32)
    live_slots = ((slot_ids % RB) < receiver_counts[owner_slab]).astype(jnp.float32)
    images = lax.map(lambda shot_inputs: one_shot(courant_sq, shot_inputs, receiver_index, live_slots), (wave_now, wave_prev, adjoint_now, adjoint_prev, source_cells, wavelet, observed))
    return -2.0 / velocity ** 3 * jnp.sum(images, axis=0)
```

```python
import jax
import jax.numpy as jnp
from jax import lax
from jax.sharding import PartitionSpec as P

TAPS = (-205.0 / 72.0, 8.0 / 5.0, -1.0 / 5.0, 8.0 / 315.0, -1.0 / 560.0)
COURANT = 0.09
RADIUS = 4


def exchange_edges(block):
    count = lax.axis_size("space")
    forward = [(i, i + 1) for i in range(count - 1)]
    backward = [(target, source) for source, target in forward]
    low = lax.ppermute(block[block.shape[0] - RADIUS :], "space", forward)
    high = lax.ppermute(block[:RADIUS], "space", backward)
    return low, high


def inner_laplace(block):
    length_x, extent_y, extent_z = block.shape
    padded = jnp.pad(block, ((4, 4), (4, 4), (4, 4)))
    result = 3.0 * TAPS[0] * block
    for distance in range(1, 5):
        beside_all = (
            padded[4 + distance : 4 + distance + length_x, 4 : 4 + extent_y, 4 : 4 + extent_z]
            + padded[4 - distance : 4 - distance + length_x, 4 : 4 + extent_y, 4 : 4 + extent_z]
        )
        beside_all = (
            beside_all
            + padded[4 : 4 + length_x, 4 + distance : 4 + distance + extent_y, 4 : 4 + extent_z]
            + padded[4 : 4 + length_x, 4 - distance : 4 - distance + extent_y, 4 : 4 + extent_z]
        )
        beside_all = (
            beside_all
            + padded[4 : 4 + length_x, 4 : 4 + extent_y, 4 + distance : 4 + distance + extent_z]
            + padded[4 : 4 + length_x, 4 : 4 + extent_y, 4 - distance : 4 - distance + extent_z]
        )
        result = result + TAPS[distance] * beside_all
    return result


def edge_terms(low, high, length_x):
    middle = jnp.zeros((length_x,) + low.shape[1:], low.dtype)
    widened = jnp.concatenate([low, middle, high], axis=0)
    result = None
    for distance in range(1, 5):
        beside = (
            widened[4 + distance : 4 + distance + length_x]
            + widened[4 - distance : 4 - distance + length_x]
        )
        term = TAPS[distance] * beside
        result = term if result is None else result + term
    return result


def step(current, former, courant_sq, injected):
    low, high = exchange_edges(current)
    interior = inner_laplace(current)
    lap = interior + edge_terms(low, high, current.shape[0])
    return 2.0 * current - former + courant_sq * lap + injected


def per_device(
    velocity,
    wave_now,
    wave_prev,
    adjoint_now,
    adjoint_prev,
    source_cells,
    wavelet,
    receiver_cells,
    receiver_counts,
    observed,
):
    extent_x, extent_y, extent_z = velocity.shape
    block_cells = extent_x * extent_y * extent_z
    steps = wavelet.shape[1]
    courant_sq = (COURANT * velocity) ** 2
    position = lax.axis_index("space")
    local_sources = source_cells[0] - position * block_cells
    inside = (local_sources >= 0) & (local_sources < block_cells)
    source_index = jnp.where(inside, local_sources, 0)
    pulses = wavelet[0]
    empty_flat = jnp.zeros((block_cells,), jnp.float32)

    current, former = wave_now[0], wave_prev[0]
    accelerations = []
    traces = []
    for t in range(steps):
        injected = empty_flat.at[source_index].add(jnp.where(inside, pulses[t], 0.0))
        latest = step(current, former, courant_sq, injected.reshape(velocity.shape))
        accelerations.append(latest - 2.0 * current + former)
        traces.append(latest.reshape(-1)[receiver_cells])
        current, former = latest, current

    live_slots = (jnp.arange(receiver_cells.shape[0], dtype=jnp.int32) < receiver_counts[0]).astype(
        jnp.float32
    )
    misfit = [(traces[t] - observed[0, t]) * live_slots for t in range(steps)]

    following, furthest = adjoint_now[0], adjoint_prev[0]
    imaging = jnp.zeros_like(velocity)
    for t in reversed(range(steps)):
        injected = empty_flat.at[receiver_cells].add(misfit[t])
        earlier = step(following, furthest, courant_sq, injected.reshape(velocity.shape))
        imaging = imaging + earlier * accelerations[t]
        following, furthest = earlier, following

    shots = lax.axis_size("shot")
    shot = lax.axis_index("shot")
    band_rows = extent_y // shots
    core = shot % 2
    half = shot // 2
    banded = imaging.reshape(extent_x, 2, 2, band_rows, extent_z)
    kept = lax.dynamic_index_in_dim(banded, core, axis=2, keepdims=False)
    sent = lax.dynamic_index_in_dim(banded, 1 - core, axis=2, keepdims=False)
    summed = kept + lax.ppermute(sent, "shot", [(s, s ^ 1) for s in range(shots)])
    kept = lax.dynamic_index_in_dim(summed, half, axis=1, keepdims=False)
    sent = lax.dynamic_index_in_dim(summed, 1 - half, axis=1, keepdims=False)
    own_band = kept + lax.ppermute(sent, "shot", [(s, s ^ 2) for s in range(shots)])

    offset = shot * band_rows
    factor = lax.dynamic_slice_in_dim(-2.0 / velocity**3, offset, band_rows, 1)
    return factor * own_band


def solution(mesh):
    in_specs = (
        P("space", None, None),
        P("shot", "space", None, None),
        P("shot", "space", None, None),
        P("shot", "space", None, None),
        P("shot", "space", None, None),
        P("shot", None),
        P("shot", None, None),
        P("space"),
        P("space"),
        P("shot", None, "space"),
    )
    out_specs = P("space", "shot", None)
    return jax.shard_map(
        per_device, mesh=mesh, in_specs=in_specs, out_specs=out_specs, check_vma=False
    )
```

```python
import jax
import jax.numpy as jnp
from jax import lax
from jax.sharding import PartitionSpec as P

TAPS = (-205.0 / 72.0, 8.0 / 5.0, -1.0 / 5.0, 8.0 / 315.0, -1.0 / 560.0)
COURANT = 0.09
RADIUS = 4


def exchange_edges(block):
    count = lax.axis_size("space")
    forward = [(i, i + 1) for i in range(count - 1)]
    backward = [(target, source) for source, target in forward]
    low = lax.ppermute(block[block.shape[0] - RADIUS :], "space", forward)
    high = lax.ppermute(block[:RADIUS], "space", backward)
    return low, high


def inner_laplace(block):
    length_x, extent_y, extent_z = block.shape
    padded = jnp.pad(block, ((4, 4), (4, 4), (4, 4)))
    result = 3.0 * TAPS[0] * block
    for distance in range(1, 5):
        beside_all = (
            padded[4 + distance : 4 + distance + length_x, 4 : 4 + extent_y, 4 : 4 + extent_z]
            + padded[4 - distance : 4 - distance + length_x, 4 : 4 + extent_y, 4 : 4 + extent_z]
        )
        beside_all = (
            beside_all
            + padded[4 : 4 + length_x, 4 + distance : 4 + distance + extent_y, 4 : 4 + extent_z]
            + padded[4 : 4 + length_x, 4 - distance : 4 - distance + extent_y, 4 : 4 + extent_z]
        )
        beside_all = (
            beside_all
            + padded[4 : 4 + length_x, 4 : 4 + extent_y, 4 + distance : 4 + distance + extent_z]
            + padded[4 : 4 + length_x, 4 : 4 + extent_y, 4 - distance : 4 - distance + extent_z]
        )
        result = result + TAPS[distance] * beside_all
    return result


def edge_terms(low, high, length_x):
    middle = jnp.zeros((length_x,) + low.shape[1:], low.dtype)
    widened = jnp.concatenate([low, middle, high], axis=0)
    result = None
    for distance in range(1, 5):
        beside = (
            widened[4 + distance : 4 + distance + length_x]
            + widened[4 - distance : 4 - distance + length_x]
        )
        term = TAPS[distance] * beside
        result = term if result is None else result + term
    return result


def step(current, former, courant_sq, injected):
    low, high = exchange_edges(current)
    interior = lax.optimization_barrier(inner_laplace(current))
    lap = interior + edge_terms(low, high, current.shape[0])
    return lax.optimization_barrier(2.0 * current - former + courant_sq * lap + injected)


def per_device(
    velocity,
    wave_now,
    wave_prev,
    adjoint_now,
    adjoint_prev,
    source_cells,
    wavelet,
    receiver_cells,
    receiver_counts,
    observed,
):
    extent_x, extent_y, extent_z = velocity.shape
    block_cells = extent_x * extent_y * extent_z
    steps = wavelet.shape[1]
    courant_sq = (COURANT * velocity) ** 2
    position = lax.axis_index("space")
    local_sources = source_cells[0] - position * block_cells
    inside = (local_sources >= 0) & (local_sources < block_cells)
    source_index = jnp.where(inside, local_sources, 0)
    pulses = wavelet[0]
    empty_flat = jnp.zeros((block_cells,), jnp.float32)
    step_ids = jnp.broadcast_to(jnp.arange(steps, dtype=jnp.int32)[:, None], pulses.shape)
    sources_all = (
        jnp.zeros((steps, block_cells), jnp.float32)
        .at[step_ids, jnp.broadcast_to(source_index, pulses.shape)]
        .add(jnp.where(inside, pulses, 0.0))
        .reshape((steps,) + velocity.shape)
    )

    current, former = wave_now[0], wave_prev[0]
    accelerations = []
    traces = []
    for t in range(steps):
        latest = step(current, former, courant_sq, sources_all[t])
        accelerations.append(lax.optimization_barrier(latest - 2.0 * current + former))
        traces.append(latest.reshape(-1)[receiver_cells])
        current, former = latest, current

    live_slots = (jnp.arange(receiver_cells.shape[0], dtype=jnp.int32) < receiver_counts[0]).astype(
        jnp.float32
    )
    misfit = [(traces[t] - observed[0, t]) * live_slots for t in range(steps)]

    following, furthest = adjoint_now[0], adjoint_prev[0]
    imaging = jnp.zeros_like(velocity)
    for t in reversed(range(steps)):
        injected = empty_flat.at[receiver_cells].add(misfit[t])
        earlier = step(following, furthest, courant_sq, injected.reshape(velocity.shape))
        imaging = lax.optimization_barrier(imaging + earlier * accelerations[t])
        following, furthest = earlier, following

    shots = lax.axis_size("shot")
    shot = lax.axis_index("shot")
    band_rows = extent_y // shots
    core = shot % 2
    half = shot // 2
    banded = imaging.reshape(extent_x, 2, 2, band_rows, extent_z)
    kept = lax.dynamic_index_in_dim(banded, core, axis=2, keepdims=False)
    sent = lax.dynamic_index_in_dim(banded, 1 - core, axis=2, keepdims=False)
    summed = kept + lax.ppermute(sent, "shot", [(s, s ^ 1) for s in range(shots)])
    kept = lax.dynamic_index_in_dim(summed, half, axis=1, keepdims=False)
    sent = lax.dynamic_index_in_dim(summed, 1 - half, axis=1, keepdims=False)
    own_band = kept + lax.ppermute(sent, "shot", [(s, s ^ 2) for s in range(shots)])

    offset = shot * band_rows
    factor = lax.dynamic_slice_in_dim(-2.0 / velocity**3, offset, band_rows, 1)
    return factor * own_band


def solution(mesh):
    in_specs = (
        P("space", None, None),
        P("shot", "space", None, None),
        P("shot", "space", None, None),
        P("shot", "space", None, None),
        P("shot", "space", None, None),
        P("shot", None),
        P("shot", None, None),
        P("space"),
        P("space"),
        P("shot", None, "space"),
    )
    out_specs = P("space", "shot", None)
    return jax.shard_map(
        per_device, mesh=mesh, in_specs=in_specs, out_specs=out_specs, check_vma=False
    )
```

```python
import jax
import jax.numpy as jnp
from jax import lax
from jax.experimental import pallas as pl
from jax.experimental.pallas import tpu as pltpu
from jax.sharding import PartitionSpec as P

TAPS = (-205.0 / 72.0, 8.0 / 5.0, -1.0 / 5.0, 8.0 / 315.0, -1.0 / 560.0)
COURANT = 0.09
RADIUS = 4


def exchange_edges(block):
    count = lax.axis_size("space")
    forward = [(i, i + 1) for i in range(count - 1)]
    backward = [(target, source) for source, target in forward]
    low = lax.ppermute(block[block.shape[0] - RADIUS :], "space", forward)
    high = lax.ppermute(block[:RADIUS], "space", backward)
    return low, high


def inner_laplace(block):
    length_x, extent_y, extent_z = block.shape
    padded = jnp.pad(block, ((4, 4), (4, 4), (4, 4)))
    result = 3.0 * TAPS[0] * block
    for distance in range(1, 5):
        beside_all = (
            padded[4 + distance : 4 + distance + length_x, 4 : 4 + extent_y, 4 : 4 + extent_z]
            + padded[4 - distance : 4 - distance + length_x, 4 : 4 + extent_y, 4 : 4 + extent_z]
        )
        beside_all = (
            beside_all
            + padded[4 : 4 + length_x, 4 + distance : 4 + distance + extent_y, 4 : 4 + extent_z]
            + padded[4 : 4 + length_x, 4 - distance : 4 - distance + extent_y, 4 : 4 + extent_z]
        )
        beside_all = (
            beside_all
            + padded[4 : 4 + length_x, 4 : 4 + extent_y, 4 + distance : 4 + distance + extent_z]
            + padded[4 : 4 + length_x, 4 : 4 + extent_y, 4 - distance : 4 - distance + extent_z]
        )
        result = result + TAPS[distance] * beside_all
    return result


def edge_terms(low, high, length_x):
    middle = jnp.zeros((length_x,) + low.shape[1:], low.dtype)
    widened = jnp.concatenate([low, middle, high], axis=0)
    result = None
    for distance in range(1, 5):
        beside = (
            widened[4 + distance : 4 + distance + length_x]
            + widened[4 - distance : 4 - distance + length_x]
        )
        term = TAPS[distance] * beside
        result = term if result is None else result + term
    return result


def update_kernel(current, former, courant_sq, interior, low, high, injected, latest):
    length_x = current.shape[0]
    for plane in range(length_x):
        edge = None
        for distance in range(1, 5):
            for near in (plane - distance, plane + distance):
                if near < 0:
                    term = low[near + RADIUS]
                elif near >= length_x:
                    term = high[near - length_x]
                else:
                    continue
                term = TAPS[distance] * term
                edge = term if edge is None else edge + term
        lap = interior[plane] if edge is None else interior[plane] + edge
        latest[plane] = (
            2.0 * current[plane] - former[plane] + courant_sq[plane] * lap + injected[plane]
        )


def fused_update(current, former, courant_sq, interior, low, high, injected):
    cells = current.size
    return pl.pallas_call(
        update_kernel,
        out_shape=jax.ShapeDtypeStruct(current.shape, current.dtype),
        in_specs=[pl.BlockSpec(memory_space=pltpu.VMEM)] * 7,
        out_specs=pl.BlockSpec(memory_space=pltpu.VMEM),
        cost_estimate=pl.CostEstimate(flops=12 * cells, transcendentals=0, bytes_accessed=28 * cells),
    )(current, former, courant_sq, interior, low, high, injected)


def step(current, former, courant_sq, injected):
    low, high = exchange_edges(current)
    interior = inner_laplace(current)
    return fused_update(current, former, courant_sq, interior, low, high, injected)


def per_device(
    velocity,
    wave_now,
    wave_prev,
    adjoint_now,
    adjoint_prev,
    source_cells,
    wavelet,
    receiver_cells,
    receiver_counts,
    observed,
):
    extent_x, extent_y, extent_z = velocity.shape
    block_cells = extent_x * extent_y * extent_z
    steps = wavelet.shape[1]
    courant_sq = (COURANT * velocity) ** 2
    position = lax.axis_index("space")
    local_sources = source_cells[0] - position * block_cells
    inside = (local_sources >= 0) & (local_sources < block_cells)
    source_index = jnp.where(inside, local_sources, 0)
    pulses = wavelet[0]
    empty_flat = jnp.zeros((block_cells,), jnp.float32)

    current, former = wave_now[0], wave_prev[0]
    accelerations = []
    traces = []
    for t in range(steps):
        injected = empty_flat.at[source_index].add(jnp.where(inside, pulses[t], 0.0))
        latest = step(current, former, courant_sq, injected.reshape(velocity.shape))
        accelerations.append(latest - 2.0 * current + former)
        traces.append(latest.reshape(-1)[receiver_cells])
        current, former = latest, current

    live_slots = (jnp.arange(receiver_cells.shape[0], dtype=jnp.int32) < receiver_counts[0]).astype(
        jnp.float32
    )
    misfit = [(traces[t] - observed[0, t]) * live_slots for t in range(steps)]

    following, furthest = adjoint_now[0], adjoint_prev[0]
    imaging = jnp.zeros_like(velocity)
    for t in reversed(range(steps)):
        injected = empty_flat.at[receiver_cells].add(misfit[t])
        earlier = step(following, furthest, courant_sq, injected.reshape(velocity.shape))
        imaging = imaging + earlier * accelerations[t]
        following, furthest = earlier, following

    shots = lax.axis_size("shot")
    shot = lax.axis_index("shot")
    band_rows = extent_y // shots
    core = shot % 2
    half = shot // 2
    banded = imaging.reshape(extent_x, 2, 2, band_rows, extent_z)
    kept = lax.dynamic_index_in_dim(banded, core, axis=2, keepdims=False)
    sent = lax.dynamic_index_in_dim(banded, 1 - core, axis=2, keepdims=False)
    summed = kept + lax.ppermute(sent, "shot", [(s, s ^ 1) for s in range(shots)])
    kept = lax.dynamic_index_in_dim(summed, half, axis=1, keepdims=False)
    sent = lax.dynamic_index_in_dim(summed, 1 - half, axis=1, keepdims=False)
    own_band = kept + lax.ppermute(sent, "shot", [(s, s ^ 2) for s in range(shots)])

    offset = shot * band_rows
    factor = lax.dynamic_slice_in_dim(-2.0 / velocity**3, offset, band_rows, 1)
    return factor * own_band


def solution(mesh):
    in_specs = (
        P("space", None, None),
        P("shot", "space", None, None),
        P("shot", "space", None, None),
        P("shot", "space", None, None),
        P("shot", "space", None, None),
        P("shot", None),
        P("shot", None, None),
        P("space"),
        P("space"),
        P("shot", None, "space"),
    )
    out_specs = P("space", "shot", None)
    return jax.shard_map(
        per_device, mesh=mesh, in_specs=in_specs, out_specs=out_specs, check_vma=False
    )
```

```python
import jax
import jax.numpy as jnp
from jax import lax
from jax.experimental import pallas as pl
from jax.experimental.pallas import tpu as pltpu
from jax.sharding import PartitionSpec as P

TAPS = (-205.0 / 72.0, 8.0 / 5.0, -1.0 / 5.0, 8.0 / 315.0, -1.0 / 560.0)
COURANT = 0.09
RADIUS = 4


def exchange_edges(block):
    count = lax.axis_size("space")
    forward = [(i, i + 1) for i in range(count - 1)]
    backward = [(target, source) for source, target in forward]
    low = lax.ppermute(block[block.shape[0] - RADIUS :], "space", forward)
    high = lax.ppermute(block[:RADIUS], "space", backward)
    return low, high


def inner_laplace(block):
    length_x, extent_y, extent_z = block.shape
    padded = jnp.pad(block, ((4, 4), (4, 4), (4, 4)))
    result = 3.0 * TAPS[0] * block
    for distance in range(1, 5):
        beside_all = (
            padded[4 + distance : 4 + distance + length_x, 4 : 4 + extent_y, 4 : 4 + extent_z]
            + padded[4 - distance : 4 - distance + length_x, 4 : 4 + extent_y, 4 : 4 + extent_z]
        )
        beside_all = (
            beside_all
            + padded[4 : 4 + length_x, 4 + distance : 4 + distance + extent_y, 4 : 4 + extent_z]
            + padded[4 : 4 + length_x, 4 - distance : 4 - distance + extent_y, 4 : 4 + extent_z]
        )
        beside_all = (
            beside_all
            + padded[4 : 4 + length_x, 4 : 4 + extent_y, 4 + distance : 4 + distance + extent_z]
            + padded[4 : 4 + length_x, 4 : 4 + extent_y, 4 - distance : 4 - distance + extent_z]
        )
        result = result + TAPS[distance] * beside_all
    return result


def edge_terms(low, high, length_x):
    middle = jnp.zeros((length_x,) + low.shape[1:], low.dtype)
    widened = jnp.concatenate([low, middle, high], axis=0)
    result = None
    for distance in range(1, 5):
        beside = (
            widened[4 + distance : 4 + distance + length_x]
            + widened[4 - distance : 4 - distance + length_x]
        )
        term = TAPS[distance] * beside
        result = term if result is None else result + term
    return result


def update_kernel(current, former, courant_sq, interior, low, high, injected, latest):
    length_x = current.shape[0]
    for plane in range(length_x):
        edge = None
        for distance in range(1, 5):
            for near in (plane - distance, plane + distance):
                if near < 0:
                    term = low[near + RADIUS]
                elif near >= length_x:
                    term = high[near - length_x]
                else:
                    continue
                term = TAPS[distance] * term
                edge = term if edge is None else edge + term
        lap = interior[plane] if edge is None else interior[plane] + edge
        latest[plane] = (
            2.0 * current[plane] - former[plane] + courant_sq[plane] * lap + injected[plane]
        )


def fused_update(current, former, courant_sq, interior, low, high, injected):
    cells = current.size
    return pl.pallas_call(
        update_kernel,
        out_shape=jax.ShapeDtypeStruct(current.shape, current.dtype),
        in_specs=[pl.BlockSpec(memory_space=pltpu.VMEM)] * 7,
        out_specs=pl.BlockSpec(memory_space=pltpu.VMEM),
        cost_estimate=pl.CostEstimate(flops=12 * cells, transcendentals=0, bytes_accessed=28 * cells),
    )(current, former, courant_sq, interior, low, high, injected)


def step(current, former, courant_sq, injected, held=None):
    low, high = exchange_edges(current)
    interior, held = lax.optimization_barrier((inner_laplace(current), held))
    lap = interior + edge_terms(low, high, current.shape[0])
    return 2.0 * current - former + courant_sq * lap + injected, held


def per_device(
    velocity,
    wave_now,
    wave_prev,
    adjoint_now,
    adjoint_prev,
    source_cells,
    wavelet,
    receiver_cells,
    receiver_counts,
    observed,
):
    extent_x, extent_y, extent_z = velocity.shape
    block_cells = extent_x * extent_y * extent_z
    steps = wavelet.shape[1]
    courant_sq = (COURANT * velocity) ** 2
    position = lax.axis_index("space")
    local_sources = source_cells[0] - position * block_cells
    inside = (local_sources >= 0) & (local_sources < block_cells)
    source_index = jnp.where(inside, local_sources, 0)
    pulses = wavelet[0]
    empty_flat = jnp.zeros((block_cells,), jnp.float32)

    current, former = wave_now[0], wave_prev[0]
    accelerations = []
    traces = []
    for t in range(steps):
        injected = empty_flat.at[source_index].add(jnp.where(inside, pulses[t], 0.0))
        latest, _ = step(current, former, courant_sq, injected.reshape(velocity.shape))
        accelerations.append(latest - 2.0 * current + former)
        traces.append(latest.reshape(-1)[receiver_cells])
        current, former = latest, current

    live_slots = (jnp.arange(receiver_cells.shape[0], dtype=jnp.int32) < receiver_counts[0]).astype(
        jnp.float32
    )
    misfit = [(traces[t] - observed[0, t]) * live_slots for t in range(steps)]

    following, furthest = adjoint_now[0], adjoint_prev[0]
    imaging = jnp.zeros_like(velocity)
    pending = None
    for t in reversed(range(steps)):
        injected = empty_flat.at[receiver_cells].add(misfit[t])
        earlier, pending = step(
            following, furthest, courant_sq, injected.reshape(velocity.shape), pending
        )
        if pending is not None:
            imaging = imaging + pending * accelerations[t + 1]
        pending = earlier
        following, furthest = earlier, following
    imaging = imaging + pending * accelerations[0]

    shots = lax.axis_size("shot")
    shot = lax.axis_index("shot")
    band_rows = extent_y // shots
    core = shot % 2
    half = shot // 2
    banded = imaging.reshape(extent_x, 2, 2, band_rows, extent_z)
    kept = lax.dynamic_index_in_dim(banded, core, axis=2, keepdims=False)
    sent = lax.dynamic_index_in_dim(banded, 1 - core, axis=2, keepdims=False)
    summed = kept + lax.ppermute(sent, "shot", [(s, s ^ 1) for s in range(shots)])
    kept = lax.dynamic_index_in_dim(summed, half, axis=1, keepdims=False)
    sent = lax.dynamic_index_in_dim(summed, 1 - half, axis=1, keepdims=False)
    own_band = kept + lax.ppermute(sent, "shot", [(s, s ^ 2) for s in range(shots)])

    offset = shot * band_rows
    factor = lax.dynamic_slice_in_dim(-2.0 / velocity**3, offset, band_rows, 1)
    return factor * own_band


def solution(mesh):
    in_specs = (
        P("space", None, None),
        P("shot", "space", None, None),
        P("shot", "space", None, None),
        P("shot", "space", None, None),
        P("shot", "space", None, None),
        P("shot", None),
        P("shot", None, None),
        P("space"),
        P("space"),
        P("shot", None, "space"),
    )
    out_specs = P("space", "shot", None)
    return jax.shard_map(
        per_device, mesh=mesh, in_specs=in_specs, out_specs=out_specs, check_vma=False
    )
```

```python
import jax
import jax.numpy as jnp
from jax import lax
from jax.sharding import PartitionSpec as P

TAPS = (-205.0 / 72.0, 8.0 / 5.0, -1.0 / 5.0, 8.0 / 315.0, -1.0 / 560.0)
COURANT = 0.09
RADIUS = 4


def exchange_edges(block):
    count = lax.axis_size("space")
    forward = [(i, i + 1) for i in range(count - 1)]
    backward = [(target, source) for source, target in forward]
    low = lax.ppermute(block[block.shape[0] - RADIUS :], "space", forward)
    high = lax.ppermute(block[:RADIUS], "space", backward)
    return low, high


def inner_laplace(block):
    length_x, extent_y, extent_z = block.shape
    padded = jnp.pad(block, ((4, 4), (4, 4), (4, 4)))
    result = 3.0 * TAPS[0] * block
    for distance in range(1, 5):
        beside_all = (
            padded[4 + distance : 4 + distance + length_x, 4 : 4 + extent_y, 4 : 4 + extent_z]
            + padded[4 - distance : 4 - distance + length_x, 4 : 4 + extent_y, 4 : 4 + extent_z]
        )
        beside_all = (
            beside_all
            + padded[4 : 4 + length_x, 4 + distance : 4 + distance + extent_y, 4 : 4 + extent_z]
            + padded[4 : 4 + length_x, 4 - distance : 4 - distance + extent_y, 4 : 4 + extent_z]
        )
        beside_all = (
            beside_all
            + padded[4 : 4 + length_x, 4 : 4 + extent_y, 4 + distance : 4 + distance + extent_z]
            + padded[4 : 4 + length_x, 4 : 4 + extent_y, 4 - distance : 4 - distance + extent_z]
        )
        result = result + TAPS[distance] * beside_all
    return result


def edge_terms(low, high, length_x):
    middle = jnp.zeros((length_x,) + low.shape[1:], low.dtype)
    widened = jnp.concatenate([low, middle, high], axis=0)
    result = None
    for distance in range(1, 5):
        beside = (
            widened[4 + distance : 4 + distance + length_x]
            + widened[4 - distance : 4 - distance + length_x]
        )
        term = TAPS[distance] * beside
        result = term if result is None else result + term
    return result


def sample_cells(field, cells):
    lanes = field.shape[-1]
    rows = field.reshape(-1, lanes)[cells // lanes]
    chosen = lax.broadcasted_iota(jnp.int32, rows.shape, 1) == (cells % lanes)[:, None]
    return jnp.sum(jnp.where(chosen, rows, 0.0), axis=1)


def place_cells(shape, cells, amounts):
    lanes = shape[-1]
    chosen = lax.broadcasted_iota(jnp.int32, (cells.shape[0], lanes), 1) == (cells % lanes)[:, None]
    rows = jnp.where(chosen, amounts[:, None], 0.0)
    size = 1
    for extent in shape:
        size *= extent
    flat = jnp.zeros((size // lanes, lanes), jnp.float32).at[cells // lanes].add(rows)
    return flat.reshape(shape)


def step(current, former, courant_sq, injected):
    low, high = exchange_edges(current)
    interior = lax.optimization_barrier(inner_laplace(current))
    lap = interior + edge_terms(low, high, current.shape[0])
    return lax.optimization_barrier(2.0 * current - former + courant_sq * lap + injected)


def per_device(
    velocity,
    wave_now,
    wave_prev,
    adjoint_now,
    adjoint_prev,
    source_cells,
    wavelet,
    receiver_cells,
    receiver_counts,
    observed,
):
    extent_x, extent_y, extent_z = velocity.shape
    block_cells = extent_x * extent_y * extent_z
    steps = wavelet.shape[1]
    courant_sq = (COURANT * velocity) ** 2
    position = lax.axis_index("space")
    local_sources = source_cells[0] - position * block_cells
    inside = (local_sources >= 0) & (local_sources < block_cells)
    source_index = jnp.where(inside, local_sources, 0)
    pulses = wavelet[0]

    current, former = wave_now[0], wave_prev[0]
    accelerations = []
    traces = []
    for t in range(steps):
        injected = place_cells(velocity.shape, source_index, jnp.where(inside, pulses[t], 0.0))
        latest = step(current, former, courant_sq, injected)
        accelerations.append(lax.optimization_barrier(latest - 2.0 * current + former))
        traces.append(sample_cells(latest, receiver_cells))
        current, former = latest, current

    live_slots = (jnp.arange(receiver_cells.shape[0], dtype=jnp.int32) < receiver_counts[0]).astype(
        jnp.float32
    )
    misfit = [(traces[t] - observed[0, t]) * live_slots for t in range(steps)]

    following, furthest = adjoint_now[0], adjoint_prev[0]
    imaging = jnp.zeros_like(velocity)
    for t in reversed(range(steps)):
        injected = place_cells(velocity.shape, receiver_cells, misfit[t])
        earlier = step(following, furthest, courant_sq, injected)
        imaging = lax.optimization_barrier(imaging + earlier * accelerations[t])
        following, furthest = earlier, following

    shots = lax.axis_size("shot")
    shot = lax.axis_index("shot")
    band_rows = extent_y // shots
    core = shot % 2
    half = shot // 2
    banded = imaging.reshape(extent_x, 2, 2, band_rows, extent_z)
    kept = lax.dynamic_index_in_dim(banded, core, axis=2, keepdims=False)
    sent = lax.dynamic_index_in_dim(banded, 1 - core, axis=2, keepdims=False)
    summed = kept + lax.ppermute(sent, "shot", [(s, s ^ 1) for s in range(shots)])
    kept = lax.dynamic_index_in_dim(summed, half, axis=1, keepdims=False)
    sent = lax.dynamic_index_in_dim(summed, 1 - half, axis=1, keepdims=False)
    own_band = kept + lax.ppermute(sent, "shot", [(s, s ^ 2) for s in range(shots)])

    offset = shot * band_rows
    factor = lax.dynamic_slice_in_dim(-2.0 / velocity**3, offset, band_rows, 1)
    return factor * own_band


def solution(mesh):
    in_specs = (
        P("space", None, None),
        P("shot", "space", None, None),
        P("shot", "space", None, None),
        P("shot", "space", None, None),
        P("shot", "space", None, None),
        P("shot", None),
        P("shot", None, None),
        P("space"),
        P("space"),
        P("shot", None, "space"),
    )
    out_specs = P("space", "shot", None)
    return jax.shard_map(
        per_device, mesh=mesh, in_specs=in_specs, out_specs=out_specs, check_vma=False
    )
```

```python
import jax
import jax.numpy as jnp
from jax import lax
from jax.sharding import PartitionSpec as P

TAPS = (-205.0 / 72.0, 8.0 / 5.0, -1.0 / 5.0, 8.0 / 315.0, -1.0 / 560.0)
COURANT = 0.09
RADIUS = 4


def exchange_edges(block):
    count = lax.axis_size("space")
    forward = [(i, i + 1) for i in range(count - 1)]
    backward = [(target, source) for source, target in forward]
    low = lax.ppermute(block[block.shape[0] - RADIUS :], "space", forward)
    high = lax.ppermute(block[:RADIUS], "space", backward)
    return low, high


def inner_laplace(block):
    length_x, extent_y, extent_z = block.shape
    padded = jnp.pad(block, ((4, 4), (4, 4), (4, 4)))
    result = 3.0 * TAPS[0] * block
    for distance in range(1, 5):
        beside_all = (
            padded[4 + distance : 4 + distance + length_x, 4 : 4 + extent_y, 4 : 4 + extent_z]
            + padded[4 - distance : 4 - distance + length_x, 4 : 4 + extent_y, 4 : 4 + extent_z]
        )
        beside_all = (
            beside_all
            + padded[4 : 4 + length_x, 4 + distance : 4 + distance + extent_y, 4 : 4 + extent_z]
            + padded[4 : 4 + length_x, 4 - distance : 4 - distance + extent_y, 4 : 4 + extent_z]
        )
        beside_all = (
            beside_all
            + padded[4 : 4 + length_x, 4 : 4 + extent_y, 4 + distance : 4 + distance + extent_z]
            + padded[4 : 4 + length_x, 4 : 4 + extent_y, 4 - distance : 4 - distance + extent_z]
        )
        result = result + TAPS[distance] * beside_all
    return result


def edge_terms(low, high, length_x):
    middle = jnp.zeros((length_x,) + low.shape[1:], low.dtype)
    widened = jnp.concatenate([low, middle, high], axis=0)
    result = None
    for distance in range(1, 5):
        beside = (
            widened[4 + distance : 4 + distance + length_x]
            + widened[4 - distance : 4 - distance + length_x]
        )
        term = TAPS[distance] * beside
        result = term if result is None else result + term
    return result


def sample_cells(field, cells):
    lanes = field.shape[-1]
    rows = field.reshape(-1, lanes)[cells // lanes]
    chosen = lax.broadcasted_iota(jnp.int32, rows.shape, 1) == (cells % lanes)[:, None]
    return jnp.sum(jnp.where(chosen, rows, 0.0), axis=1)


def place_cells(shape, cells, amounts):
    lanes = shape[-1]
    chosen = lax.broadcasted_iota(jnp.int32, (cells.shape[0], lanes), 1) == (cells % lanes)[:, None]
    rows = jnp.where(chosen, amounts[:, None], 0.0)
    size = 1
    for extent in shape:
        size *= extent
    flat = jnp.zeros((size // lanes, lanes), jnp.float32).at[cells // lanes].add(rows)
    return flat.reshape(shape)


def step(current, former, courant_sq, injected):
    low, high = exchange_edges(current)
    base = lax.optimization_barrier(
        2.0 * current - former + courant_sq * inner_laplace(current) + injected
    )
    return lax.optimization_barrier(base + courant_sq * edge_terms(low, high, current.shape[0]))


def per_device(
    velocity,
    wave_now,
    wave_prev,
    adjoint_now,
    adjoint_prev,
    source_cells,
    wavelet,
    receiver_cells,
    receiver_counts,
    observed,
):
    extent_x, extent_y, extent_z = velocity.shape
    block_cells = extent_x * extent_y * extent_z
    steps = wavelet.shape[1]
    courant_sq = (COURANT * velocity) ** 2
    position = lax.axis_index("space")
    local_sources = source_cells[0] - position * block_cells
    inside = (local_sources >= 0) & (local_sources < block_cells)
    source_index = jnp.where(inside, local_sources, 0)
    pulses = wavelet[0]

    current, former = wave_now[0], wave_prev[0]
    accelerations = []
    traces = []
    for t in range(steps):
        injected = place_cells(velocity.shape, source_index, jnp.where(inside, pulses[t], 0.0))
        latest = step(current, former, courant_sq, injected)
        accelerations.append(lax.optimization_barrier(latest - 2.0 * current + former))
        traces.append(sample_cells(latest, receiver_cells))
        current, former = latest, current

    live_slots = (jnp.arange(receiver_cells.shape[0], dtype=jnp.int32) < receiver_counts[0]).astype(
        jnp.float32
    )
    misfit = [(traces[t] - observed[0, t]) * live_slots for t in range(steps)]

    following, furthest = adjoint_now[0], adjoint_prev[0]
    imaging = jnp.zeros_like(velocity)
    for t in reversed(range(steps)):
        injected = place_cells(velocity.shape, receiver_cells, misfit[t])
        earlier = step(following, furthest, courant_sq, injected)
        imaging = lax.optimization_barrier(imaging + earlier * accelerations[t])
        following, furthest = earlier, following

    shots = lax.axis_size("shot")
    shot = lax.axis_index("shot")
    band_rows = extent_y // shots
    core = shot % 2
    half = shot // 2
    banded = imaging.reshape(extent_x, 2, 2, band_rows, extent_z)
    kept = lax.dynamic_index_in_dim(banded, core, axis=2, keepdims=False)
    sent = lax.dynamic_index_in_dim(banded, 1 - core, axis=2, keepdims=False)
    summed = kept + lax.ppermute(sent, "shot", [(s, s ^ 1) for s in range(shots)])
    kept = lax.dynamic_index_in_dim(summed, half, axis=1, keepdims=False)
    sent = lax.dynamic_index_in_dim(summed, 1 - half, axis=1, keepdims=False)
    own_band = kept + lax.ppermute(sent, "shot", [(s, s ^ 2) for s in range(shots)])

    offset = shot * band_rows
    factor = lax.dynamic_slice_in_dim(-2.0 / velocity**3, offset, band_rows, 1)
    return factor * own_band


def solution(mesh):
    in_specs = (
        P("space", None, None),
        P("shot", "space", None, None),
        P("shot", "space", None, None),
        P("shot", "space", None, None),
        P("shot", "space", None, None),
        P("shot", None),
        P("shot", None, None),
        P("space"),
        P("space"),
        P("shot", None, "space"),
    )
    out_specs = P("space", "shot", None)
    return jax.shard_map(
        per_device, mesh=mesh, in_specs=in_specs, out_specs=out_specs, check_vma=False
    )
```

```python
import jax
import jax.numpy as jnp
from jax import lax
from jax.sharding import PartitionSpec as P

TAPS = (-205.0 / 72.0, 8.0 / 5.0, -1.0 / 5.0, 8.0 / 315.0, -1.0 / 560.0)
COURANT = 0.09
RADIUS = 4


def exchange_edges(block):
    count = lax.axis_size("space")
    forward = [(i, i + 1) for i in range(count - 1)]
    backward = [(target, source) for source, target in forward]
    low = lax.ppermute(block[block.shape[0] - RADIUS :], "space", forward)
    high = lax.ppermute(block[:RADIUS], "space", backward)
    return low, high


def inner_laplace(block):
    length_x, extent_y, extent_z = block.shape
    padded = jnp.pad(block, ((4, 4), (4, 4), (4, 4)))
    result = 3.0 * TAPS[0] * block
    for distance in range(1, 5):
        beside_all = (
            padded[4 + distance : 4 + distance + length_x, 4 : 4 + extent_y, 4 : 4 + extent_z]
            + padded[4 - distance : 4 - distance + length_x, 4 : 4 + extent_y, 4 : 4 + extent_z]
        )
        beside_all = (
            beside_all
            + padded[4 : 4 + length_x, 4 + distance : 4 + distance + extent_y, 4 : 4 + extent_z]
            + padded[4 : 4 + length_x, 4 - distance : 4 - distance + extent_y, 4 : 4 + extent_z]
        )
        beside_all = (
            beside_all
            + padded[4 : 4 + length_x, 4 : 4 + extent_y, 4 + distance : 4 + distance + extent_z]
            + padded[4 : 4 + length_x, 4 : 4 + extent_y, 4 - distance : 4 - distance + extent_z]
        )
        result = result + TAPS[distance] * beside_all
    return result


def edge_terms(low, high, length_x):
    middle = jnp.zeros((length_x,) + low.shape[1:], low.dtype)
    widened = jnp.concatenate([low, middle, high], axis=0)
    result = None
    for distance in range(1, 5):
        beside = (
            widened[4 + distance : 4 + distance + length_x]
            + widened[4 - distance : 4 - distance + length_x]
        )
        term = TAPS[distance] * beside
        result = term if result is None else result + term
    return result


def sample_cells(field, cells):
    lanes = field.shape[-1]
    rows = field.reshape(-1, lanes)[cells // lanes]
    chosen = lax.broadcasted_iota(jnp.int32, rows.shape, 1) == (cells % lanes)[:, None]
    return jnp.sum(jnp.where(chosen, rows, 0.0), axis=1)


def place_cells(shape, cells, amounts):
    lanes = shape[-1]
    size = 1
    for extent in shape:
        size *= extent
    rows = lax.broadcasted_iota(jnp.int32, (size // lanes, cells.shape[0]), 0)
    by_row = jnp.where(rows == (cells // lanes)[None, :], amounts[None, :], 0.0)
    columns = lax.broadcasted_iota(jnp.int32, (cells.shape[0], lanes), 1)
    by_lane = (columns == (cells % lanes)[:, None]).astype(jnp.float32)
    placed = jnp.dot(by_row, by_lane, precision=lax.Precision.HIGHEST)
    return placed.reshape(shape)


def step(current, former, courant_sq, injected):
    low, high = exchange_edges(current)
    base = lax.optimization_barrier(
        2.0 * current - former + courant_sq * inner_laplace(current) + injected
    )
    return lax.optimization_barrier(base + courant_sq * edge_terms(low, high, current.shape[0]))


def per_device(
    velocity,
    wave_now,
    wave_prev,
    adjoint_now,
    adjoint_prev,
    source_cells,
    wavelet,
    receiver_cells,
    receiver_counts,
    observed,
):
    extent_x, extent_y, extent_z = velocity.shape
    block_cells = extent_x * extent_y * extent_z
    steps = wavelet.shape[1]
    courant_sq = (COURANT * velocity) ** 2
    position = lax.axis_index("space")
    local_sources = source_cells[0] - position * block_cells
    inside = (local_sources >= 0) & (local_sources < block_cells)
    source_index = jnp.where(inside, local_sources, 0)
    pulses = wavelet[0]

    current, former = wave_now[0], wave_prev[0]
    accelerations = []
    traces = []
    for t in range(steps):
        injected = place_cells(velocity.shape, source_index, jnp.where(inside, pulses[t], 0.0))
        latest = step(current, former, courant_sq, injected)
        accelerations.append(lax.optimization_barrier(latest - 2.0 * current + former))
        traces.append(sample_cells(latest, receiver_cells))
        current, former = latest, current

    live_slots = (jnp.arange(receiver_cells.shape[0], dtype=jnp.int32) < receiver_counts[0]).astype(
        jnp.float32
    )
    misfit = [(traces[t] - observed[0, t]) * live_slots for t in range(steps)]

    following, furthest = adjoint_now[0], adjoint_prev[0]
    imaging = jnp.zeros_like(velocity)
    for t in reversed(range(steps)):
        injected = place_cells(velocity.shape, receiver_cells, misfit[t])
        earlier = step(following, furthest, courant_sq, injected)
        imaging = lax.optimization_barrier(imaging + earlier * accelerations[t])
        following, furthest = earlier, following

    shots = lax.axis_size("shot")
    shot = lax.axis_index("shot")
    band_rows = extent_y // shots
    core = shot % 2
    half = shot // 2
    banded = imaging.reshape(extent_x, 2, 2, band_rows, extent_z)
    kept = lax.dynamic_index_in_dim(banded, core, axis=2, keepdims=False)
    sent = lax.dynamic_index_in_dim(banded, 1 - core, axis=2, keepdims=False)
    summed = kept + lax.ppermute(sent, "shot", [(s, s ^ 1) for s in range(shots)])
    kept = lax.dynamic_index_in_dim(summed, half, axis=1, keepdims=False)
    sent = lax.dynamic_index_in_dim(summed, 1 - half, axis=1, keepdims=False)
    own_band = kept + lax.ppermute(sent, "shot", [(s, s ^ 2) for s in range(shots)])

    offset = shot * band_rows
    factor = lax.dynamic_slice_in_dim(-2.0 / velocity**3, offset, band_rows, 1)
    return factor * own_band


def solution(mesh):
    in_specs = (
        P("space", None, None),
        P("shot", "space", None, None),
        P("shot", "space", None, None),
        P("shot", "space", None, None),
        P("shot", "space", None, None),
        P("shot", None),
        P("shot", None, None),
        P("space"),
        P("space"),
        P("shot", None, "space"),
    )
    out_specs = P("space", "shot", None)
    return jax.shard_map(
        per_device, mesh=mesh, in_specs=in_specs, out_specs=out_specs, check_vma=False
    )
```

```python
import jax
import jax.numpy as jnp
from jax import lax
from jax.sharding import PartitionSpec as P

TAPS = (-205.0 / 72.0, 8.0 / 5.0, -1.0 / 5.0, 8.0 / 315.0, -1.0 / 560.0)
COURANT = 0.09
RADIUS = 4


def exchange_edges(block):
    count = lax.axis_size("space")
    forward = [(i, i + 1) for i in range(count - 1)]
    backward = [(target, source) for source, target in forward]
    low = lax.ppermute(block[block.shape[0] - RADIUS :], "space", forward)
    high = lax.ppermute(block[:RADIUS], "space", backward)
    return low, high


def inner_laplace(block):
    length_x, extent_y, extent_z = block.shape
    padded = jnp.pad(block, ((4, 4), (4, 4), (4, 4)))
    result = 3.0 * TAPS[0] * block
    for distance in range(1, 5):
        beside_all = (
            padded[4 + distance : 4 + distance + length_x, 4 : 4 + extent_y, 4 : 4 + extent_z]
            + padded[4 - distance : 4 - distance + length_x, 4 : 4 + extent_y, 4 : 4 + extent_z]
        )
        beside_all = (
            beside_all
            + padded[4 : 4 + length_x, 4 + distance : 4 + distance + extent_y, 4 : 4 + extent_z]
            + padded[4 : 4 + length_x, 4 - distance : 4 - distance + extent_y, 4 : 4 + extent_z]
        )
        beside_all = (
            beside_all
            + padded[4 : 4 + length_x, 4 : 4 + extent_y, 4 + distance : 4 + distance + extent_z]
            + padded[4 : 4 + length_x, 4 : 4 + extent_y, 4 - distance : 4 - distance + extent_z]
        )
        result = result + TAPS[distance] * beside_all
    return result


def edge_terms(low, high, length_x):
    middle = jnp.zeros((length_x,) + low.shape[1:], low.dtype)
    widened = jnp.concatenate([low, middle, high], axis=0)
    result = None
    for distance in range(1, 5):
        beside = (
            widened[4 + distance : 4 + distance + length_x]
            + widened[4 - distance : 4 - distance + length_x]
        )
        term = TAPS[distance] * beside
        result = term if result is None else result + term
    return result


def sample_cells(field, cells):
    lanes = field.shape[-1]
    rows = field.reshape(-1, lanes)[cells // lanes]
    chosen = lax.broadcasted_iota(jnp.int32, rows.shape, 1) == (cells % lanes)[:, None]
    return jnp.sum(jnp.where(chosen, rows, 0.0), axis=1)


def place_cells(shape, cells, amounts):
    lanes = shape[-1]
    size = 1
    for extent in shape:
        size *= extent
    rows = lax.broadcasted_iota(jnp.int32, (size // lanes, cells.shape[0]), 0)
    by_row = jnp.where(rows == (cells // lanes)[None, :], amounts[None, :], 0.0)
    columns = lax.broadcasted_iota(jnp.int32, (cells.shape[0], lanes), 1)
    by_lane = (columns == (cells % lanes)[:, None]).astype(jnp.float32)
    placed = jnp.dot(by_row, by_lane, precision=lax.Precision.HIGHEST)
    return placed.reshape(shape)


def step(current, former, courant_sq, injected):
    low, high = exchange_edges(current)
    base = lax.optimization_barrier(
        2.0 * current - former + courant_sq * inner_laplace(current) + injected
    )
    return lax.optimization_barrier(base + courant_sq * edge_terms(low, high, current.shape[0]))


def per_device(
    velocity,
    wave_now,
    wave_prev,
    adjoint_now,
    adjoint_prev,
    source_cells,
    wavelet,
    receiver_cells,
    receiver_counts,
    observed,
):
    extent_x, extent_y, extent_z = velocity.shape
    block_cells = extent_x * extent_y * extent_z
    steps = wavelet.shape[1]
    courant_sq = (COURANT * velocity) ** 2
    position = lax.axis_index("space")
    local_sources = source_cells[0] - position * block_cells
    inside = (local_sources >= 0) & (local_sources < block_cells)
    source_index = jnp.where(inside, local_sources, 0)
    pulses = wavelet[0]

    current, former = wave_now[0], wave_prev[0]
    accelerations = []
    traces = []
    for t in range(steps):
        amounts, _ = lax.optimization_barrier((jnp.where(inside, pulses[t], 0.0), current))
        injected = place_cells(velocity.shape, source_index, amounts)
        latest = step(current, former, courant_sq, injected)
        accelerations.append(lax.optimization_barrier(latest - 2.0 * current + former))
        traces.append(sample_cells(latest, receiver_cells))
        current, former = latest, current

    live_slots = (jnp.arange(receiver_cells.shape[0], dtype=jnp.int32) < receiver_counts[0]).astype(
        jnp.float32
    )
    misfit = [(traces[t] - observed[0, t]) * live_slots for t in range(steps)]

    following, furthest = adjoint_now[0], adjoint_prev[0]
    imaging = jnp.zeros_like(velocity)
    for t in reversed(range(steps)):
        amounts, _ = lax.optimization_barrier((misfit[t], following))
        injected = place_cells(velocity.shape, receiver_cells, amounts)
        earlier = step(following, furthest, courant_sq, injected)
        imaging = lax.optimization_barrier(imaging + earlier * accelerations[t])
        following, furthest = earlier, following

    shots = lax.axis_size("shot")
    shot = lax.axis_index("shot")
    band_rows = extent_y // shots
    core = shot % 2
    half = shot // 2
    banded = imaging.reshape(extent_x, 2, 2, band_rows, extent_z)
    kept = lax.dynamic_index_in_dim(banded, core, axis=2, keepdims=False)
    sent = lax.dynamic_index_in_dim(banded, 1 - core, axis=2, keepdims=False)
    summed = kept + lax.ppermute(sent, "shot", [(s, s ^ 1) for s in range(shots)])
    kept = lax.dynamic_index_in_dim(summed, half, axis=1, keepdims=False)
    sent = lax.dynamic_index_in_dim(summed, 1 - half, axis=1, keepdims=False)
    own_band = kept + lax.ppermute(sent, "shot", [(s, s ^ 2) for s in range(shots)])

    offset = shot * band_rows
    factor = lax.dynamic_slice_in_dim(-2.0 / velocity**3, offset, band_rows, 1)
    return factor * own_band


def solution(mesh):
    in_specs = (
        P("space", None, None),
        P("shot", "space", None, None),
        P("shot", "space", None, None),
        P("shot", "space", None, None),
        P("shot", "space", None, None),
        P("shot", None),
        P("shot", None, None),
        P("space"),
        P("space"),
        P("shot", None, "space"),
    )
    out_specs = P("space", "shot", None)
    return jax.shard_map(
        per_device, mesh=mesh, in_specs=in_specs, out_specs=out_specs, check_vma=False
    )
```

```python
import jax
import jax.numpy as jnp
from jax import lax
from jax.sharding import PartitionSpec as P

TAPS = (-205.0 / 72.0, 8.0 / 5.0, -1.0 / 5.0, 8.0 / 315.0, -1.0 / 560.0)
COURANT = 0.09
RADIUS = 4


def exchange_edges(block):
    count = lax.axis_size("space")
    forward = [(i, i + 1) for i in range(count - 1)]
    backward = [(target, source) for source, target in forward]
    low = lax.ppermute(block[block.shape[0] - RADIUS :], "space", forward)
    high = lax.ppermute(block[:RADIUS], "space", backward)
    return low, high


def inner_laplace(block):
    length_x, extent_y, extent_z = block.shape
    padded = jnp.pad(block, ((4, 4), (4, 4), (4, 4)))
    result = 3.0 * TAPS[0] * block
    for distance in range(1, 5):
        beside_all = (
            padded[4 + distance : 4 + distance + length_x, 4 : 4 + extent_y, 4 : 4 + extent_z]
            + padded[4 - distance : 4 - distance + length_x, 4 : 4 + extent_y, 4 : 4 + extent_z]
        )
        beside_all = (
            beside_all
            + padded[4 : 4 + length_x, 4 + distance : 4 + distance + extent_y, 4 : 4 + extent_z]
            + padded[4 : 4 + length_x, 4 - distance : 4 - distance + extent_y, 4 : 4 + extent_z]
        )
        beside_all = (
            beside_all
            + padded[4 : 4 + length_x, 4 : 4 + extent_y, 4 + distance : 4 + distance + extent_z]
            + padded[4 : 4 + length_x, 4 : 4 + extent_y, 4 - distance : 4 - distance + extent_z]
        )
        result = result + TAPS[distance] * beside_all
    return result


def edge_terms(low, high, length_x):
    middle = jnp.zeros((length_x,) + low.shape[1:], low.dtype)
    widened = jnp.concatenate([low, middle, high], axis=0)
    result = None
    for distance in range(1, 5):
        beside = (
            widened[4 + distance : 4 + distance + length_x]
            + widened[4 - distance : 4 - distance + length_x]
        )
        term = TAPS[distance] * beside
        result = term if result is None else result + term
    return result


def sample_cells(field, cells):
    lanes = field.shape[-1]
    rows = field.reshape(-1, lanes)[cells // lanes]
    chosen = lax.broadcasted_iota(jnp.int32, rows.shape, 1) == (cells % lanes)[:, None]
    return jnp.sum(jnp.where(chosen, rows, 0.0), axis=1)


def place_cells(shape, cells, amounts):
    lanes = shape[-1]
    size = 1
    for extent in shape:
        size *= extent
    rows = lax.broadcasted_iota(jnp.int32, (size // lanes, cells.shape[0]), 0)
    by_row = jnp.where(rows == (cells // lanes)[None, :], amounts[None, :], 0.0)
    columns = lax.broadcasted_iota(jnp.int32, (cells.shape[0], lanes), 1)
    by_lane = (columns == (cells % lanes)[:, None]).astype(jnp.float32)
    placed = jnp.dot(by_row, by_lane, precision=lax.Precision.HIGHEST)
    return placed.reshape(shape)


def step(current, former, courant_sq, injected):
    low, high = exchange_edges(current)
    base = lax.optimization_barrier(
        2.0 * current - former + courant_sq * inner_laplace(current) + injected
    )
    return lax.optimization_barrier(base + courant_sq * edge_terms(low, high, current.shape[0]))


def per_device(
    velocity,
    wave_now,
    wave_prev,
    adjoint_now,
    adjoint_prev,
    source_cells,
    wavelet,
    receiver_cells,
    receiver_counts,
    observed,
):
    extent_x, extent_y, extent_z = velocity.shape
    block_cells = extent_x * extent_y * extent_z
    steps = wavelet.shape[1]
    courant_sq = (COURANT * velocity) ** 2
    position = lax.axis_index("space")
    local_sources = source_cells[0] - position * block_cells
    inside = (local_sources >= 0) & (local_sources < block_cells)
    source_index = jnp.where(inside, local_sources, 0)
    pulses = wavelet[0]

    lanes = extent_z
    row_ids = lax.broadcasted_iota(jnp.int32, (steps, block_cells // lanes, pulses.shape[1]), 1)
    by_row = jnp.where(
        row_ids == (source_index // lanes)[None, None, :],
        jnp.where(inside, pulses, 0.0)[:, None, :],
        0.0,
    ).reshape(-1, pulses.shape[1])
    lane_ids = lax.broadcasted_iota(jnp.int32, (pulses.shape[1], lanes), 1)
    by_lane = (lane_ids == (source_index % lanes)[:, None]).astype(jnp.float32)
    sources_all = jnp.dot(by_row, by_lane, precision=lax.Precision.HIGHEST).reshape(
        (steps,) + velocity.shape
    )

    current, former = wave_now[0], wave_prev[0]
    accelerations = []
    traces = []
    for t in range(steps):
        latest = step(current, former, courant_sq, sources_all[t])
        accelerations.append(lax.optimization_barrier(latest - 2.0 * current + former))
        traces.append(sample_cells(latest, receiver_cells))
        current, former = latest, current

    live_slots = (jnp.arange(receiver_cells.shape[0], dtype=jnp.int32) < receiver_counts[0]).astype(
        jnp.float32
    )
    misfit = [(traces[t] - observed[0, t]) * live_slots for t in range(steps)]

    following, furthest = adjoint_now[0], adjoint_prev[0]
    imaging = jnp.zeros_like(velocity)
    for t in reversed(range(steps)):
        injected = place_cells(velocity.shape, receiver_cells, misfit[t])
        earlier = step(following, furthest, courant_sq, injected)
        imaging = lax.optimization_barrier(imaging + earlier * accelerations[t])
        following, furthest = earlier, following

    shots = lax.axis_size("shot")
    shot = lax.axis_index("shot")
    band_rows = extent_y // shots
    core = shot % 2
    half = shot // 2
    banded = imaging.reshape(extent_x, 2, 2, band_rows, extent_z)
    kept = lax.dynamic_index_in_dim(banded, core, axis=2, keepdims=False)
    sent = lax.dynamic_index_in_dim(banded, 1 - core, axis=2, keepdims=False)
    summed = kept + lax.ppermute(sent, "shot", [(s, s ^ 1) for s in range(shots)])
    kept = lax.dynamic_index_in_dim(summed, half, axis=1, keepdims=False)
    sent = lax.dynamic_index_in_dim(summed, 1 - half, axis=1, keepdims=False)
    own_band = kept + lax.ppermute(sent, "shot", [(s, s ^ 2) for s in range(shots)])

    offset = shot * band_rows
    factor = lax.dynamic_slice_in_dim(-2.0 / velocity**3, offset, band_rows, 1)
    return factor * own_band


def solution(mesh):
    in_specs = (
        P("space", None, None),
        P("shot", "space", None, None),
        P("shot", "space", None, None),
        P("shot", "space", None, None),
        P("shot", "space", None, None),
        P("shot", None),
        P("shot", None, None),
        P("space"),
        P("space"),
        P("shot", None, "space"),
    )
    out_specs = P("space", "shot", None)
    return jax.shard_map(
        per_device, mesh=mesh, in_specs=in_specs, out_specs=out_specs, check_vma=False
    )
```

```python
import jax
import jax.numpy as jnp
from jax import lax
from jax.sharding import PartitionSpec as P

TAPS = (-205.0 / 72.0, 8.0 / 5.0, -1.0 / 5.0, 8.0 / 315.0, -1.0 / 560.0)
COURANT = 0.09
RADIUS = 4


def unused_exchange_edges(block):
    count = lax.axis_size("space")
    forward = [(i, i + 1) for i in range(count - 1)]
    backward = [(target, source) for source, target in forward]
    low = lax.ppermute(block[block.shape[0] - RADIUS :], "space", forward)
    high = lax.ppermute(block[:RADIUS], "space", backward)
    return low, high


def inner_laplace(block):
    length_x, extent_y, extent_z = block.shape
    padded = jnp.pad(block, ((4, 4), (4, 4), (4, 4)))
    result = 3.0 * TAPS[0] * block
    for distance in range(1, 5):
        beside_all = (
            padded[4 + distance : 4 + distance + length_x, 4 : 4 + extent_y, 4 : 4 + extent_z]
            + padded[4 - distance : 4 - distance + length_x, 4 : 4 + extent_y, 4 : 4 + extent_z]
        )
        beside_all = (
            beside_all
            + padded[4 : 4 + length_x, 4 + distance : 4 + distance + extent_y, 4 : 4 + extent_z]
            + padded[4 : 4 + length_x, 4 - distance : 4 - distance + extent_y, 4 : 4 + extent_z]
        )
        beside_all = (
            beside_all
            + padded[4 : 4 + length_x, 4 : 4 + extent_y, 4 + distance : 4 + distance + extent_z]
            + padded[4 : 4 + length_x, 4 : 4 + extent_y, 4 - distance : 4 - distance + extent_z]
        )
        result = result + TAPS[distance] * beside_all
    return result


def edge_terms(low, high, length_x):
    middle = jnp.zeros((length_x,) + low.shape[1:], low.dtype)
    widened = jnp.concatenate([low, middle, high], axis=0)
    result = None
    for distance in range(1, 5):
        beside = (
            widened[4 + distance : 4 + distance + length_x]
            + widened[4 - distance : 4 - distance + length_x]
        )
        term = TAPS[distance] * beside
        result = term if result is None else result + term
    return result


def sample_cells(field, cells):
    lanes = field.shape[-1]
    rows = field.reshape(-1, lanes)[cells // lanes]
    chosen = lax.broadcasted_iota(jnp.int32, rows.shape, 1) == (cells % lanes)[:, None]
    return jnp.sum(jnp.where(chosen, rows, 0.0), axis=1)


def place_cells(shape, cells, amounts):
    lanes = shape[-1]
    size = 1
    for extent in shape:
        size *= extent
    rows = lax.broadcasted_iota(jnp.int32, (size // lanes, cells.shape[0]), 0)
    by_row = jnp.where(rows == (cells // lanes)[None, :], amounts[None, :], 0.0)
    columns = lax.broadcasted_iota(jnp.int32, (cells.shape[0], lanes), 1)
    by_lane = (columns == (cells % lanes)[:, None]).astype(jnp.float32)
    placed = jnp.dot(by_row, by_lane, precision=lax.Precision.HIGHEST)
    return placed.reshape(shape)


def low_edge_terms(low):
    planes = []
    for plane in range(RADIUS):
        total = None
        for distance in range(plane + 1, RADIUS + 1):
            term = TAPS[distance] * low[RADIUS + plane - distance]
            total = term if total is None else total + term
        planes.append(total)
    return jnp.stack(planes)


def high_edge_terms(high):
    planes = []
    for plane in range(RADIUS):
        total = None
        for distance in range(RADIUS - plane, RADIUS + 1):
            term = TAPS[distance] * high[plane + distance - RADIUS]
            total = term if total is None else total + term
        planes.append(total)
    return jnp.stack(planes)


def step(lower, upper, former, courant_sq, injected):
    count = lax.axis_size("space")
    forward = [(i, i + 1) for i in range(count - 1)]
    backward = [(target, source) for source, target in forward]
    low = lax.ppermute(upper, "space", forward)
    high = lax.ppermute(lower, "space", backward)
    current = jnp.concatenate([lower, upper], axis=0)
    base = lax.optimization_barrier(
        2.0 * current - former + courant_sq * inner_laplace(current) + injected
    )
    new_lower = lax.optimization_barrier(
        base[:RADIUS] + courant_sq[:RADIUS] * low_edge_terms(low)
    )
    new_upper = lax.optimization_barrier(
        base[RADIUS:] + courant_sq[RADIUS:] * high_edge_terms(high)
    )
    return new_lower, new_upper


def per_device(
    velocity,
    wave_now,
    wave_prev,
    adjoint_now,
    adjoint_prev,
    source_cells,
    wavelet,
    receiver_cells,
    receiver_counts,
    observed,
):
    extent_x, extent_y, extent_z = velocity.shape
    block_cells = extent_x * extent_y * extent_z
    steps = wavelet.shape[1]
    courant_sq = (COURANT * velocity) ** 2
    position = lax.axis_index("space")
    local_sources = source_cells[0] - position * block_cells
    inside = (local_sources >= 0) & (local_sources < block_cells)
    source_index = jnp.where(inside, local_sources, 0)
    pulses = wavelet[0]

    assert extent_x == 2 * RADIUS
    lower, upper, former = wave_now[0, :RADIUS], wave_now[0, RADIUS:], wave_prev[0]
    accelerations = []
    traces = []
    for t in range(steps):
        injected = place_cells(velocity.shape, source_index, jnp.where(inside, pulses[t], 0.0))
        current = jnp.concatenate([lower, upper], axis=0)
        lower, upper = step(lower, upper, former, courant_sq, injected)
        latest = jnp.concatenate([lower, upper], axis=0)
        accelerations.append(lax.optimization_barrier(latest - 2.0 * current + former))
        traces.append(sample_cells(latest, receiver_cells))
        former = current

    live_slots = (jnp.arange(receiver_cells.shape[0], dtype=jnp.int32) < receiver_counts[0]).astype(
        jnp.float32
    )
    misfit = [(traces[t] - observed[0, t]) * live_slots for t in range(steps)]

    lower, upper, furthest = adjoint_now[0, :RADIUS], adjoint_now[0, RADIUS:], adjoint_prev[0]
    imaging = jnp.zeros_like(velocity)
    for t in reversed(range(steps)):
        injected = place_cells(velocity.shape, receiver_cells, misfit[t])
        following = jnp.concatenate([lower, upper], axis=0)
        lower, upper = step(lower, upper, furthest, courant_sq, injected)
        earlier = jnp.concatenate([lower, upper], axis=0)
        imaging = lax.optimization_barrier(imaging + earlier * accelerations[t])
        furthest = following

    shots = lax.axis_size("shot")
    shot = lax.axis_index("shot")
    band_rows = extent_y // shots
    core = shot % 2
    half = shot // 2
    banded = imaging.reshape(extent_x, 2, 2, band_rows, extent_z)
    kept = lax.dynamic_index_in_dim(banded, core, axis=2, keepdims=False)
    sent = lax.dynamic_index_in_dim(banded, 1 - core, axis=2, keepdims=False)
    summed = kept + lax.ppermute(sent, "shot", [(s, s ^ 1) for s in range(shots)])
    kept = lax.dynamic_index_in_dim(summed, half, axis=1, keepdims=False)
    sent = lax.dynamic_index_in_dim(summed, 1 - half, axis=1, keepdims=False)
    own_band = kept + lax.ppermute(sent, "shot", [(s, s ^ 2) for s in range(shots)])

    offset = shot * band_rows
    factor = lax.dynamic_slice_in_dim(-2.0 / velocity**3, offset, band_rows, 1)
    return factor * own_band


def solution(mesh):
    in_specs = (
        P("space", None, None),
        P("shot", "space", None, None),
        P("shot", "space", None, None),
        P("shot", "space", None, None),
        P("shot", "space", None, None),
        P("shot", None),
        P("shot", None, None),
        P("space"),
        P("space"),
        P("shot", None, "space"),
    )
    out_specs = P("space", "shot", None)
    return jax.shard_map(
        per_device, mesh=mesh, in_specs=in_specs, out_specs=out_specs, check_vma=False
    )
```

```python
import jax
import jax.numpy as jnp
from jax import lax
from jax.sharding import PartitionSpec as P

TAPS = (-205.0 / 72.0, 8.0 / 5.0, -1.0 / 5.0, 8.0 / 315.0, -1.0 / 560.0)
COURANT = 0.09
RADIUS = 4


def exchange_edges(block):
    count = lax.axis_size("space")
    forward = [(i, i + 1) for i in range(count - 1)]
    backward = [(target, source) for source, target in forward]
    low = lax.ppermute(block[block.shape[0] - RADIUS :], "space", forward)
    high = lax.ppermute(block[:RADIUS], "space", backward)
    return low, high


def inner_laplace(block):
    length_x, extent_y, extent_z = block.shape
    padded = jnp.pad(block, ((4, 4), (4, 4), (4, 4)))
    result = 3.0 * TAPS[0] * block
    for distance in range(1, 5):
        beside_all = (
            padded[4 + distance : 4 + distance + length_x, 4 : 4 + extent_y, 4 : 4 + extent_z]
            + padded[4 - distance : 4 - distance + length_x, 4 : 4 + extent_y, 4 : 4 + extent_z]
        )
        beside_all = (
            beside_all
            + padded[4 : 4 + length_x, 4 + distance : 4 + distance + extent_y, 4 : 4 + extent_z]
            + padded[4 : 4 + length_x, 4 - distance : 4 - distance + extent_y, 4 : 4 + extent_z]
        )
        beside_all = (
            beside_all
            + padded[4 : 4 + length_x, 4 : 4 + extent_y, 4 + distance : 4 + distance + extent_z]
            + padded[4 : 4 + length_x, 4 : 4 + extent_y, 4 - distance : 4 - distance + extent_z]
        )
        result = result + TAPS[distance] * beside_all
    return result


def edge_terms(low, high, length_x):
    middle = jnp.zeros((length_x,) + low.shape[1:], low.dtype)
    widened = jnp.concatenate([low, middle, high], axis=0)
    result = None
    for distance in range(1, 5):
        beside = (
            widened[4 + distance : 4 + distance + length_x]
            + widened[4 - distance : 4 - distance + length_x]
        )
        term = TAPS[distance] * beside
        result = term if result is None else result + term
    return result


def sample_cells(field, cells):
    lanes = field.shape[-1]
    rows = field.reshape(-1, lanes)[cells // lanes]
    chosen = lax.broadcasted_iota(jnp.int32, rows.shape, 1) == (cells % lanes)[:, None]
    return jnp.sum(jnp.where(chosen, rows, 0.0), axis=1)


def place_cells(shape, cells, amounts):
    lanes = shape[-1]
    size = 1
    for extent in shape:
        size *= extent
    rows = lax.broadcasted_iota(jnp.int32, (size // lanes, cells.shape[0]), 0)
    by_row = jnp.where(rows == (cells // lanes)[None, :], amounts[None, :], 0.0)
    columns = lax.broadcasted_iota(jnp.int32, (cells.shape[0], lanes), 1)
    by_lane = (columns == (cells % lanes)[:, None]).astype(jnp.float32)
    placed = jnp.dot(by_row, by_lane, precision=lax.Precision.HIGHEST)
    return placed.reshape(shape)


def step(current, former, courant_sq, injected):
    low, high = exchange_edges(current)
    base = lax.optimization_barrier(
        2.0 * current - former + courant_sq * inner_laplace(current) + injected
    )
    return lax.optimization_barrier(base + courant_sq * edge_terms(low, high, current.shape[0]))


def per_device(
    velocity,
    wave_now,
    wave_prev,
    adjoint_now,
    adjoint_prev,
    source_cells,
    wavelet,
    receiver_cells,
    receiver_counts,
    observed,
):
    extent_x, extent_y, extent_z = velocity.shape
    block_cells = extent_x * extent_y * extent_z
    steps = wavelet.shape[1]
    courant_sq = (COURANT * velocity) ** 2
    position = lax.axis_index("space")
    local_sources = source_cells[0] - position * block_cells
    inside = (local_sources >= 0) & (local_sources < block_cells)
    source_index = jnp.where(inside, local_sources, 0)
    pulses = wavelet[0]

    current, former = wave_now[0], wave_prev[0]
    accelerations = []
    traces = []
    for t in range(steps):
        if t == steps - 1:
            last_start = current
        injected = place_cells(velocity.shape, source_index, jnp.where(inside, pulses[t], 0.0))
        latest = step(current, former, courant_sq, injected)
        accelerations.append(lax.optimization_barrier(latest - 2.0 * current + former))
        traces.append(sample_cells(latest, receiver_cells))
        current, former = latest, current

    live_slots = (jnp.arange(receiver_cells.shape[0], dtype=jnp.int32) < receiver_counts[0]).astype(
        jnp.float32
    )
    misfit = [(traces[t] - observed[0, t]) * live_slots for t in range(steps)]

    following, _ = lax.optimization_barrier((adjoint_now[0], last_start))
    furthest = adjoint_prev[0]
    imaging = jnp.zeros_like(velocity)
    for t in reversed(range(steps)):
        injected = place_cells(velocity.shape, receiver_cells, misfit[t])
        earlier = step(following, furthest, courant_sq, injected)
        imaging = lax.optimization_barrier(imaging + earlier * accelerations[t])
        following, furthest = earlier, following

    shots = lax.axis_size("shot")
    shot = lax.axis_index("shot")
    band_rows = extent_y // shots
    core = shot % 2
    half = shot // 2
    banded = imaging.reshape(extent_x, 2, 2, band_rows, extent_z)
    kept = lax.dynamic_index_in_dim(banded, core, axis=2, keepdims=False)
    sent = lax.dynamic_index_in_dim(banded, 1 - core, axis=2, keepdims=False)
    summed = kept + lax.ppermute(sent, "shot", [(s, s ^ 1) for s in range(shots)])
    kept = lax.dynamic_index_in_dim(summed, half, axis=1, keepdims=False)
    sent = lax.dynamic_index_in_dim(summed, 1 - half, axis=1, keepdims=False)
    own_band = kept + lax.ppermute(sent, "shot", [(s, s ^ 2) for s in range(shots)])

    offset = shot * band_rows
    factor = lax.dynamic_slice_in_dim(-2.0 / velocity**3, offset, band_rows, 1)
    return factor * own_band


def solution(mesh):
    in_specs = (
        P("space", None, None),
        P("shot", "space", None, None),
        P("shot", "space", None, None),
        P("shot", "space", None, None),
        P("shot", "space", None, None),
        P("shot", None),
        P("shot", None, None),
        P("space"),
        P("space"),
        P("shot", None, "space"),
    )
    out_specs = P("space", "shot", None)
    return jax.shard_map(
        per_device, mesh=mesh, in_specs=in_specs, out_specs=out_specs, check_vma=False
    )
```
